32 devices in a mesh: groups: 2 (over x), lon: 16 (over z, y, core).
Axes of the slice: x: 2, y: 2, z: 4, core: 2. Of those that a mesh axis runs over, the one named last changes fastest.
Arguments:
- fields: bfloat16 [128, 512, 256], P('groups', 'lon'), parts along dimension 0, may hold values from -36 to 36
- sea_mask: int32 [128, 512], P('groups', 'lon'), parts along dimension 0, may hold values 0 or 1
- cotangent: bfloat16 [128, 512, 256], P('groups', 'lon'), parts along dimension 0, may hold values from -6 to 6
- depth_kernel: float32 [7, 7, 256], replicated, may hold values from -0.875 to 0.875
- norm_gain: float32 [256], replicated, may hold values from 0.1 to 1.9
- up_weight: bfloat16 [256, 1024], replicated, may hold values from -0.375 to 0.375
- down_weight: bfloat16 [256, 1024], replicated, may hold values from -0.1875 to 0.1875
- layer_scale: float32 [256], replicated, may hold values from 0.3 to 3
Outputs:
- grad_fields: bfloat16 [128, 512, 256], P('groups', 'lon'), parts along dimension 0
- grad_kernel: float32 [14, 7, 256], P('groups'), parts along dimension 0
- grad_up: float32 [256, 2048], P('lon', 'groups'), parts along dimension 1
- grad_down: float32 [256, 2048], P('lon', 'groups'), parts along dimension 1
The draws below stay inside these ranges and needn't reach their ends.
There are 2 independent parts, one for each index of `groups`. The reference program is written for one: setup_inputs(seed, part) draws one part's arguments, and reference() takes and returns one part's arrays. A program takes and returns all parts, laid end to end along the dimension named above; an argument that names none is the same for every part. Nothing has to cross between parts.
All inputs are finite; a program needn't handle non-finite values. No bound on the sum of `sea_mask` on one device may be relied on, other than what follows from the above.
Results may differ from the reference program's by a relative error of at most 0.0063.
Values may be sent and summed in bfloat16 or wider, within the bound.
A program may use at most 128 MiB of HBM per device.

```python
import math
import jax
import jax.numpy as jnp
from jax import lax

C = 256
HID = 1024
LAT = 64
NX = 512


def draw_fields(key, part):
    base_key = jax.random.fold_in(key, 101)
    key_base, key_cell, key_chan = jax.random.split(base_key, 3)
    base = jnp.clip(jax.random.normal(key_base, (LAT, NX, C), jnp.float32), -4.0, 4.0)
    cell_scale = jnp.exp(jax.random.uniform(key_cell, (LAT, NX, 1), jnp.float32, math.log(0.3), math.log(3.0)))
    chan_scale = jnp.exp(jax.random.uniform(key_chan, (1, 1, C), jnp.float32, math.log(0.3), math.log(3.0)))
    return (base * cell_scale * chan_scale).astype(jnp.bfloat16)


def with_ends(array, own_key, smallest, top_value):
    spot = [jax.random.randint(jax.random.fold_in(own_key, axis), (), 0, length) for axis, length in enumerate(array.shape)]
    widest = array.shape.index(max(array.shape))
    neighbour = spot[:widest] + [(spot[widest] + 1) % array.shape[widest]] + spot[widest + 1:]
    return array.at[tuple(spot)].set(smallest).at[tuple(neighbour)].set(top_value)


def with_spikes(result, rng, source, target, parts, factor):
    owner, partner = [(jnp.arange(result.shape[position]) // (result.shape[position] // parts)).reshape([-1 if axis == position else 1 for axis in range(result.ndim)]) for position in (source, target)]
    chosen = jax.random.permutation(rng, parts)[partner]
    strong = (owner == chosen) | (owner == (partner + parts // 2) % parts)
    return jnp.where(strong, factor * result, result)


def steps_of(own_key, extent, cuts, smallest, largest):
    loudness = 1.0
    for axis_at, shards_of in cuts:
        draws = jax.random.uniform(jax.random.fold_in(jax.random.fold_in(own_key, 6), axis_at), (shards_of,), jnp.float32, smallest / len(cuts), largest / len(cuts))
        loudness = loudness * jnp.repeat(jnp.exp(draws), extent[axis_at] // shards_of).reshape((-1,) + (1,) * (len(extent) - 1 - axis_at))
    return loudness


def scatter_about(own_key, dims, width, limit, cuts=(), kind=jnp.bfloat16):
    values = width * jax.random.normal(own_key, dims, jnp.float32)
    if cuts:
        values = values * steps_of(own_key, dims, cuts, -0.22, 0.18)
    return jnp.clip(values, -limit, limit).astype(kind)


def gaussian_with(stream_key, shape, width, limit, pieces, heavy, held_as=jnp.bfloat16):
    result = width * jax.random.normal(stream_key, shape, jnp.float32)
    if pieces:
        result = result * steps_of(stream_key, shape, pieces, -0.22, 0.18)
    return jnp.clip(with_spikes(result, jax.random.fold_in(stream_key, 3), *heavy), -limit, limit).astype(held_as)


def setup_inputs(seed: int = 0, part: int = 0) -> dict:
    streams_of = jax.random.split(jax.random.key(seed), 9)
    own_keys = jax.random.split(jax.random.fold_in(streams_of[8], part), 9)
    return {
        "fields": draw_fields(jax.random.fold_in(jax.random.fold_in(streams_of[8], part), 71), part),
        "sea_mask": with_ends((jax.random.randint(own_keys[1], (LAT, NX), 0, 4) < 3).astype(jnp.int32), jax.random.fold_in(own_keys[1], 1), 0, 1),
        "cotangent": gaussian_with(own_keys[2], (LAT, NX, C), 1.0, 6.0, ((1, 16),), (1, 2, 16, 2.0)),
        "depth_kernel": scatter_about(streams_of[3], (7, 7, C), 49 ** -0.5, 0.875, (), jnp.float32),
        "norm_gain": jnp.clip(1.0 + 0.18 * jax.random.normal(streams_of[4], (C,), jnp.float32), 0.1, 1.9),
        "up_weight": scatter_about(streams_of[5], (C, HID), C ** -0.5, 0.375),
        "down_weight": scatter_about(streams_of[6], (C, HID), HID ** -0.5, 0.1875),
        "layer_scale": jnp.clip(jnp.exp(jax.random.uniform(streams_of[7], (C,), jnp.float32, math.log(0.3), math.log(3.0))), 0.3, 3.0),
    }


def gelu_tanh(values):
    return jax.nn.gelu(values, approximate=True)

def reference(fields, sea_mask, cotangent, depth_kernel, norm_gain, up_weight, down_weight, layer_scale):
    band_rows = LAT
    band_cols = NX
    mask_bf = sea_mask.astype(jnp.bfloat16)[:, :, None]
    masked = fields * mask_bf
    ghost = masked[band_rows - 3:][::-1, ::-1]
    south = jnp.zeros((3, band_cols, C), jnp.bfloat16)
    padded = jnp.concatenate([south, masked, ghost], axis=0)
    extended = jnp.concatenate([padded[:, band_cols - 3:], padded, padded[:, :3]], axis=1)
    ext_wide = extended.astype(jnp.float32)
    conv = jnp.zeros((band_rows, band_cols, C), jnp.float32)
    for row_tap in range(7):
        for col_tap in range(7):
            conv = conv + depth_kernel[row_tap, col_tap] * ext_wide[row_tap:row_tap + band_rows, col_tap:col_tap + band_cols]
    mean_z = lax.optimization_barrier(jnp.mean(conv, axis=-1, keepdims=True))
    centred = conv - mean_z
    inv_std = lax.rsqrt(lax.optimization_barrier(jnp.mean(centred * centred, axis=-1, keepdims=True)) + 1e-06)
    nhat = centred * inv_std
    normed = (nhat * norm_gain).astype(jnp.bfloat16)
    dout = (cotangent.astype(jnp.float32) * layer_scale * mask_bf.astype(jnp.float32)).astype(jnp.bfloat16)
    factor = 1.0 / math.sqrt(band_rows * band_cols)
    contract_rows = (((0,), (0,)), ((), ()))
    contract_cols = (((1,), (1,)), ((), ()))

    def row_step(carry, inputs):
        normed_row, dout_row = inputs
        preact = jnp.dot(normed_row, up_weight, preferred_element_type=jnp.float32)
        hidden = gelu_tanh(preact).astype(jnp.bfloat16)
        dhid = jnp.dot(dout_row, down_weight, preferred_element_type=jnp.float32)
        _, back = jax.vjp(gelu_tanh, preact)
        dpre = back(dhid)[0].astype(jnp.bfloat16)
        dnorm = lax.dot_general(dpre, up_weight, contract_cols, preferred_element_type=jnp.float32)
        grad_up = carry[0] + lax.dot_general(normed_row, dpre, contract_rows, preferred_element_type=jnp.float32)
        grad_down = carry[1] + lax.dot_general(dout_row, hidden, contract_rows, preferred_element_type=jnp.float32)
        return ((grad_up, grad_down), dnorm)
    start = (jnp.zeros((C, HID), jnp.float32), jnp.zeros((C, HID), jnp.float32))
    (grad_up, grad_down), dnorm = lax.scan(row_step, start, (normed, dout))
    scaled = dnorm * norm_gain
    grad_conv = inv_std * (scaled - lax.optimization_barrier(jnp.mean(scaled, axis=-1, keepdims=True)) - nhat * lax.optimization_barrier(jnp.mean(scaled * nhat, axis=-1, keepdims=True)))
    taps = []
    for row_tap in range(7):
        for col_tap in range(7):
            taps.append(lax.optimization_barrier(jnp.sum(grad_conv * ext_wide[row_tap:row_tap + band_rows, col_tap:col_tap + band_cols], axis=(0, 1))))
    grad_kernel = jnp.stack(taps, axis=0).reshape(7, 7, C) * factor
    grad_pad = jnp.pad(grad_conv, ((6, 6), (6, 6), (0, 0)))
    grad_ext = jnp.zeros((band_rows + 6, band_cols + 6, C), jnp.float32)
    for row_tap in range(7):
        for col_tap in range(7):
            grad_ext = grad_ext + depth_kernel[row_tap, col_tap] * grad_pad[6 - row_tap:12 - row_tap + band_rows, 6 - col_tap:12 - col_tap + band_cols]
    grad_padded = grad_ext[:, 3:band_cols + 3]
    grad_padded = grad_padded.at[:, :3].add(grad_ext[:, band_cols + 3:])
    grad_padded = grad_padded.at[:, band_cols - 3:].add(grad_ext[:, :3])
    grad_masked = grad_padded[3:band_rows + 3]
    grad_masked = grad_masked.at[band_rows - 3:].add(grad_padded[band_rows + 3:][::-1, ::-1])
    grad_fields = (cotangent.astype(jnp.float32) + mask_bf.astype(jnp.float32) * grad_masked).astype(jnp.bfloat16)
    return (grad_fields, grad_kernel, grad_up * factor, grad_down * factor)
```

```python
import functools
import math

import jax
import jax.numpy as jnp
from jax import lax
from jax.experimental import pallas as pl
from jax.experimental.pallas import tpu as pltpu
from jax.sharding import PartitionSpec as P

VMEM_LIMIT = 56 * 1024 * 1024
ROOT = math.sqrt(2.0 / math.pi)


def halo(block, count):
    cols = block.shape[1]
    seam = block[block.shape[0] - 3 :]
    left = lax.ppermute(block[:, cols - 3 :], "lon", [(i, (i + 1) % count) for i in range(count)])
    right = lax.ppermute(block[:, :3], "lon", [((i + 1) % count, i) for i in range(count)])
    middle = lax.ppermute(seam, "lon", [(i, count - 1 - i) for i in range(count)])
    before = lax.ppermute(seam[:, :3], "lon", [(i, (count - i) % count) for i in range(count)])
    after = lax.ppermute(
        seam[:, cols - 3 :], "lon", [(i, (2 * count - 2 - i) % count) for i in range(count)]
    )
    ghost = jnp.concatenate([before[:, ::-1], middle[:, ::-1], after[:, ::-1]], axis=1)[::-1]
    return left, right, ghost


def framed(block, left, right, ghost):
    rows, cols, channels = block.shape
    wide = jnp.float32
    body = jnp.concatenate([left.astype(wide), block.astype(wide), right.astype(wide)], axis=1)
    full = jnp.concatenate(
        [jnp.zeros((3, cols + 6, channels), wide), body, ghost.astype(wide)], axis=0
    )
    return jnp.pad(full, ((0, 0), (0, 2), (0, 0)))


def shift_into(source, shifted, rows, cols):
    for col_tap in range(7):

        @pl.loop(0, rows // 2)
        def _(step):
            at = pl.ds(step * 2, 2)
            shifted[col_tap, at] = source[at, col_tap : col_tap + cols, :]


def conv_block(shifted, taps, row, col, lanes, flip):
    total = [jnp.zeros((8, 128), jnp.float32) for _ in range(8)]
    for b in range(7):
        cells = [shifted[b, row + i, pl.ds(col, 8), lanes] for i in range(14)]
        for a in range(7):
            tap = taps[(6 - a) * 7 + 6 - b if flip else a * 7 + b, :, lanes]
            for j in range(8):
                total[j] = total[j] + tap * cells[j + a]
    return total


def forward_kernel(ext, taps, nhat, istd, shifted):
    rows, cols, channels = nhat.shape
    shift_into(ext, shifted, rows + 6, cols)

    @pl.loop(0, (rows // 8) * (cols // 8))
    def _(step):
        row = (step // (cols // 8)) * 8
        col = pl.multiple_of((step % (cols // 8)) * 8, 8)
        halves = [
            conv_block(shifted, taps, row, col, slice(128 * h, 128 * h + 128), False)
            for h in range(channels // 128)
        ]
        for j in range(8):
            parts = [half[j] for half in halves]
            mean = sum(jnp.sum(p, axis=-1, keepdims=True) for p in parts) / channels
            centred = [p - mean for p in parts]
            var = sum(jnp.sum(p * p, axis=-1, keepdims=True) for p in centred) / channels
            inv = lax.rsqrt(var + 1e-06)
            istd[row + j, pl.ds(col, 8), :] = inv
            for h, p in enumerate(centred):
                nhat[row + j, pl.ds(col, 8), 128 * h : 128 * h + 128] = p * inv


def mlp_kernel(
    factor, nhat, istd, mask, cot, gain, scale, up, down, grad, terms, sum_up, sum_down
):
    step = pl.program_id(0)
    hidden_width = up.shape[1]

    @pl.when(step == 0)
    def _():
        sum_up[...] = jnp.zeros_like(sum_up)
        sum_down[...] = jnp.zeros_like(sum_down)

    wide = jnp.float32
    nh = nhat[...]
    normed = (nh * gain[...]).astype(jnp.bfloat16)
    dout = (cot[...].astype(wide) * scale[...] * mask[...]).astype(jnp.bfloat16)
    rows_of = (((0,), (0,)), ((), ()))
    cols_of = (((1,), (1,)), ((), ()))
    dnorm = jnp.zeros(nh.shape, wide)
    part = 512
    for at in range(0, hidden_width, part):
        piece = slice(at, at + part)
        pre = jnp.dot(normed, up[:, piece], preferred_element_type=wide)
        dhid = jnp.dot(dout, down[:, piece], preferred_element_type=wide)
        square = pre * pre
        t = jnp.tanh(pre * (ROOT + (ROOT * 0.044715) * square))
        half = 0.5 + 0.5 * t
        hidden = pre * half
        slope = half + (0.5 * pre) * (1.0 - t * t) * (ROOT + (3.0 * ROOT * 0.044715) * square)
        dpre = (dhid * slope).astype(jnp.bfloat16)
        hidden = hidden.astype(jnp.bfloat16)
        sum_up[:, piece] += lax.dot_general(normed, dpre, rows_of, preferred_element_type=wide)
        sum_down[:, piece] += lax.dot_general(dout, hidden, rows_of, preferred_element_type=wide)
        dnorm += lax.dot_general(dpre, up[:, piece], cols_of, preferred_element_type=wide)
    dn = dnorm * gain[...]
    first = jnp.mean(dn, axis=-1, keepdims=True)
    second = jnp.mean(dn * nh, axis=-1, keepdims=True)
    grad[...] = istd[...] * (dn - first - nh * second)

    @pl.when(step == pl.num_programs(0) - 1)
    def _():
        terms[:, :hidden_width] = (sum_up[...] * factor).astype(terms.dtype)
        terms[:, hidden_width:] = (sum_down[...] * factor).astype(terms.dtype)


def taps_kernel(factor, ext, grad, out, shifted):
    rows, cols, channels = grad.shape
    shift_into(ext, shifted, rows + 6, cols)

    for h in range(channels // 128):
        lanes = slice(128 * h, 128 * h + 128)
        for b in range(7):

            def body(step, total):
                row = step * 8
                total = list(total)
                for col in range(0, cols, 8):
                    there = slice(col, col + 8)
                    cells = [shifted[b, row + i, there, lanes] for i in range(14)]
                    for j in range(8):
                        value = grad[row + j, there, lanes]
                        for a in range(7):
                            total[a] = total[a] + value * cells[j + a]
                return tuple(total)

            start = tuple(jnp.zeros((8, 128), jnp.float32) for _ in range(7))
            total = lax.fori_loop(0, rows // 8, body, start)
            for a in range(7):
                out[a, b : b + 1, lanes] = factor * jnp.sum(total[a], axis=0, keepdims=True)


def back_kernel(gext, taps, mask, cot, out, shifted, summed):
    rows, cols, channels = out.shape
    shift_into(gext, shifted, rows + 6, cols)

    @pl.loop(0, cols // 8)
    def _(step):
        there = pl.ds(pl.multiple_of(step * 8, 8), 8)
        for h in range(channels // 128):
            lanes = slice(128 * h, 128 * h + 128)
            for row in range(rows - 3, rows):
                total = jnp.zeros((8, 128), jnp.float32)
                for a in range(rows + 3 - row, 7):
                    for b in range(7):
                        total = total + taps[a * 7 + b, :, lanes] * shifted[b, row + a, there, lanes]
                summed[row, there, lanes] = total

    shifted[:, rows + 3 :] = jnp.zeros((7, 3, cols, channels), jnp.float32)
    summed[: rows - 3] = jnp.zeros((rows - 3, cols, channels), jnp.float32)

    @pl.loop(0, (rows // 8) * (cols // 8))
    def _(step):
        row = (step // (cols // 8)) * 8
        col = pl.multiple_of((step % (cols // 8)) * 8, 8)
        for h in range(channels // 128):
            lanes = slice(128 * h, 128 * h + 128)
            total = conv_block(shifted, taps, row, col, lanes, True)
            for j in range(8):
                at = summed.at[row + j, pl.ds(col, 8), lanes]
                at[...] = at[...] + total[j]

    @pl.loop(0, rows // 4)
    def _(step):
        at = pl.ds(step * 4, 4)
        out[at] = (cot[at].astype(jnp.float32) + mask[at] * summed[at]).astype(out.dtype)


def local(
    fields, sea_mask, cotangent, depth_kernel, norm_gain, up_weight, down_weight, layer_scale
):
    rows, cols, channels = fields.shape
    count = lax.axis_size("lon")
    cells = rows * cols
    hidden_width = up_weight.shape[1]
    factor = 1.0 / math.sqrt(cells * count)
    wide = jnp.float32
    in_vmem = pl.BlockSpec(memory_space=pltpu.VMEM)
    params = pltpu.CompilerParams(vmem_limit_bytes=VMEM_LIMIT)
    shape = functools.partial(jax.ShapeDtypeStruct, dtype=wide)
    shifted = pltpu.VMEM((7, rows + 6, cols, channels), wide)
    conv_cost = pl.CostEstimate(
        flops=100 * cells * channels, bytes_accessed=12 * cells * channels, transcendentals=0
    )

    masked = fields * sea_mask.astype(jnp.bfloat16)[:, :, None]
    mask = sea_mask.astype(wide)[:, :, None]
    ext = framed(masked, *halo(masked, count))
    taps = jnp.broadcast_to(depth_kernel.reshape(49, 1, channels), (49, 8, channels))

    nhat, istd = pl.pallas_call(
        forward_kernel,
        out_shape=(shape((rows, cols, channels)), shape((rows, cols, 1))),
        in_specs=[in_vmem] * 2,
        out_specs=(in_vmem, in_vmem),
        scratch_shapes=[shifted],
        compiler_params=params,
        cost_estimate=conv_cost,
        name="forward_conv",
    )(ext, taps)

    tile = 256
    by_cell = pl.BlockSpec((tile, channels), lambda i: (i, 0))
    one = pl.BlockSpec((tile, 1), lambda i: (i, 0))
    whole = lambda *dims: pl.BlockSpec(dims, lambda i: (0, 0))
    grad, terms = pl.pallas_call(
        functools.partial(mlp_kernel, factor),
        grid=(cells // tile,),
        out_shape=(
            shape((cells, channels)),
            jax.ShapeDtypeStruct((channels, 2 * hidden_width), jnp.bfloat16),
        ),
        in_specs=[
            by_cell,
            one,
            one,
            by_cell,
            whole(1, channels),
            whole(1, channels),
            whole(channels, hidden_width),
            whole(channels, hidden_width),
        ],
        out_specs=(by_cell, whole(channels, 2 * hidden_width)),
        scratch_shapes=[pltpu.VMEM((channels, hidden_width), wide)] * 2,
        compiler_params=params,
        cost_estimate=pl.CostEstimate(
            flops=10 * cells * channels * hidden_width,
            bytes_accessed=12 * cells * channels,
            transcendentals=cells * hidden_width,
        ),
        name="mlp",
    )(
        nhat.reshape(cells, channels),
        istd.reshape(cells, 1),
        mask.reshape(cells, 1),
        cotangent.reshape(cells, channels),
        norm_gain.reshape(1, channels),
        layer_scale.reshape(1, channels),
        up_weight,
        down_weight,
    )
    grad = grad.reshape(rows, cols, channels)
    around = halo(grad.astype(jnp.bfloat16), count)

    local_kernel = pl.pallas_call(
        functools.partial(taps_kernel, factor),
        out_shape=shape((7, 7, channels)),
        in_specs=[in_vmem] * 2,
        out_specs=in_vmem,
        scratch_shapes=[shifted],
        compiler_params=params,
        cost_estimate=conv_cost,
        name="kernel_grad",
    )(ext, grad)

    grad_fields = pl.pallas_call(
        back_kernel,
        out_shape=jax.ShapeDtypeStruct((rows, cols, channels), jnp.bfloat16),
        in_specs=[in_vmem] * 4,
        out_specs=in_vmem,
        scratch_shapes=[shifted, pltpu.VMEM((rows, cols, channels), wide)],
        compiler_params=params,
        cost_estimate=conv_cost,
        name="back_conv",
    )(framed(grad, *around), taps, mask, cotangent)

    gathered = lax.all_gather(local_kernel, "lon")
    grad_kernel = jnp.sum(gathered, axis=0)
    arrived = lax.all_to_all(
        terms.reshape(count, channels // count, 2 * hidden_width), "lon", 0, 0
    )
    owned = jnp.sum(arrived.astype(wide), axis=0)
    return (grad_fields, grad_kernel, owned[:, :hidden_width], owned[:, hidden_width:])


def solution(mesh):
    return jax.shard_map(
        local,
        mesh=mesh,
        in_specs=(
            P("groups", "lon", None),
            P("groups", "lon"),
            P("groups", "lon", None),
            P(),
            P(),
            P(),
            P(),
            P(),
        ),
        out_specs=(
            P("groups", "lon", None),
            P("groups", None, None),
            P("lon", "groups"),
            P("lon", "groups"),
        ),
        check_vma=False,
    )
```

```python
import functools
import math

import jax
import jax.numpy as jnp
from jax import lax
from jax.experimental import pallas as pl
from jax.experimental.pallas import tpu as pltpu
from jax.sharding import PartitionSpec as P

VMEM_LIMIT = 56 * 1024 * 1024
ROOT = math.sqrt(2.0 / math.pi)


def halo(block, count):
    cols = block.shape[1]
    seam = block[block.shape[0] - 3 :]
    left = lax.ppermute(block[:, cols - 3 :], "lon", [(i, (i + 1) % count) for i in range(count)])
    right = lax.ppermute(block[:, :3], "lon", [((i + 1) % count, i) for i in range(count)])
    seam = jnp.concatenate([left[-3:], seam, right[-3:]], axis=1)
    ghost = lax.ppermute(seam, "lon", [(i, count - 1 - i) for i in range(count)])[::-1, ::-1]
    return left, right, ghost


def framed(block, left, right, ghost):
    rows, cols, channels = block.shape
    wide = jnp.float32
    body = jnp.concatenate([left.astype(wide), block.astype(wide), right.astype(wide)], axis=1)
    full = jnp.concatenate(
        [jnp.zeros((3, cols + 6, channels), wide), body, ghost.astype(wide)], axis=0
    )
    return jnp.pad(full, ((0, 0), (0, 2), (0, 0)))


def shift_into(source, shifted, rows, cols):
    for col_tap in range(7):

        @pl.loop(0, rows // 2)
        def _(step):
            at = pl.ds(step * 2, 2)
            shifted[col_tap, at] = source[at, col_tap : col_tap + cols, :]


def conv_block(shifted, taps, row, col, lanes, flip):
    total = [jnp.zeros((8, 128), jnp.float32) for _ in range(8)]
    for b in range(7):
        cells = [shifted[b, row + i, pl.ds(col, 8), lanes] for i in range(14)]
        for a in range(7):
            tap = taps[(6 - a) * 7 + 6 - b if flip else a * 7 + b, :, lanes]
            for j in range(8):
                total[j] = total[j] + tap * cells[j + a]
    return total


def forward_kernel(ext, taps, nhat, istd, shifted):
    rows, cols, channels = nhat.shape
    shift_into(ext, shifted, rows + 6, cols)

    @pl.loop(0, (rows // 8) * (cols // 8))
    def _(step):
        row = (step // (cols // 8)) * 8
        col = pl.multiple_of((step % (cols // 8)) * 8, 8)
        halves = [
            conv_block(shifted, taps, row, col, slice(128 * h, 128 * h + 128), False)
            for h in range(channels // 128)
        ]
        for j in range(8):
            parts = [half[j] for half in halves]
            mean = sum(jnp.sum(p, axis=-1, keepdims=True) for p in parts) / channels
            centred = [p - mean for p in parts]
            var = sum(jnp.sum(p * p, axis=-1, keepdims=True) for p in centred) / channels
            inv = lax.rsqrt(var + 1e-06)
            istd[row + j, pl.ds(col, 8), :] = inv
            for h, p in enumerate(centred):
                nhat[row + j, pl.ds(col, 8), 128 * h : 128 * h + 128] = p * inv


def mlp_kernel(
    factor, nhat, istd, mask, cot, gain, scale, up, down, grad, terms, sum_up, sum_down
):
    step = pl.program_id(0)
    hidden_width = up.shape[1]

    @pl.when(step == 0)
    def _():
        sum_up[...] = jnp.zeros_like(sum_up)
        sum_down[...] = jnp.zeros_like(sum_down)

    wide = jnp.float32
    nh = nhat[...]
    normed = (nh * gain[...]).astype(jnp.bfloat16)
    dout = (cot[...].astype(wide) * scale[...] * mask[...]).astype(jnp.bfloat16)
    rows_of = (((0,), (0,)), ((), ()))
    cols_of = (((1,), (1,)), ((), ()))
    dnorm = jnp.zeros(nh.shape, wide)
    part = 512
    for at in range(0, hidden_width, part):
        piece = slice(at, at + part)
        pre = jnp.dot(normed, up[:, piece], preferred_element_type=wide)
        dhid = jnp.dot(dout, down[:, piece], preferred_element_type=wide)
        square = pre * pre
        t = jnp.tanh(pre * (ROOT + (ROOT * 0.044715) * square))
        half = 0.5 + 0.5 * t
        hidden = pre * half
        slope = half + (0.5 * pre) * (1.0 - t * t) * (ROOT + (3.0 * ROOT * 0.044715) * square)
        dpre = (dhid * slope).astype(jnp.bfloat16)
        hidden = hidden.astype(jnp.bfloat16)
        sum_up[:, piece] += lax.dot_general(normed, dpre, rows_of, preferred_element_type=wide)
        sum_down[:, piece] += lax.dot_general(dout, hidden, rows_of, preferred_element_type=wide)
        dnorm += lax.dot_general(dpre, up[:, piece], cols_of, preferred_element_type=wide)
    dn = dnorm * gain[...]
    first = jnp.mean(dn, axis=-1, keepdims=True)
    second = jnp.mean(dn * nh, axis=-1, keepdims=True)
    grad[...] = istd[...] * (dn - first - nh * second)

    @pl.when(step == pl.num_programs(0) - 1)
    def _():
        terms[:, :hidden_width] = (sum_up[...] * factor).astype(terms.dtype)
        terms[:, hidden_width:] = (sum_down[...] * factor).astype(terms.dtype)


def taps_kernel(factor, ext, grad, out, shifted):
    rows, cols, channels = grad.shape
    shift_into(ext, shifted, rows + 6, cols)

    for h in range(channels // 128):
        lanes = slice(128 * h, 128 * h + 128)
        for b in range(7):

            def body(step, total):
                row = step * 8
                total = list(total)
                for col in range(0, cols, 8):
                    there = slice(col, col + 8)
                    cells = [shifted[b, row + i, there, lanes] for i in range(14)]
                    for j in range(8):
                        value = grad[row + j, there, lanes]
                        for a in range(7):
                            total[a] = total[a] + value * cells[j + a]
                return tuple(total)

            start = tuple(jnp.zeros((8, 128), jnp.float32) for _ in range(7))
            total = lax.fori_loop(0, rows // 8, body, start)
            for a in range(7):
                out[a, b : b + 1, lanes] = factor * jnp.sum(total[a], axis=0, keepdims=True)


def back_kernel(gext, taps, mask, cot, out, shifted, summed):
    rows, cols, channels = out.shape
    shift_into(gext, shifted, rows + 6, cols)

    @pl.loop(0, cols // 8)
    def _(step):
        there = pl.ds(pl.multiple_of(step * 8, 8), 8)
        for h in range(channels // 128):
            lanes = slice(128 * h, 128 * h + 128)
            for row in range(rows - 3, rows):
                total = jnp.zeros((8, 128), jnp.float32)
                for a in range(rows + 3 - row, 7):
                    for b in range(7):
                        total = total + taps[a * 7 + b, :, lanes] * shifted[b, row + a, there, lanes]
                summed[row, there, lanes] = total

    shifted[:, rows + 3 :] = jnp.zeros((7, 3, cols, channels), jnp.float32)
    summed[: rows - 3] = jnp.zeros((rows - 3, cols, channels), jnp.float32)

    @pl.loop(0, (rows // 8) * (cols // 8))
    def _(step):
        row = (step // (cols // 8)) * 8
        col = pl.multiple_of((step % (cols // 8)) * 8, 8)
        for h in range(channels // 128):
            lanes = slice(128 * h, 128 * h + 128)
            total = conv_block(shifted, taps, row, col, lanes, True)
            for j in range(8):
                at = summed.at[row + j, pl.ds(col, 8), lanes]
                at[...] = at[...] + total[j]

    @pl.loop(0, rows // 4)
    def _(step):
        at = pl.ds(step * 4, 4)
        out[at] = (cot[at].astype(jnp.float32) + mask[at] * summed[at]).astype(out.dtype)


def local(
    fields, sea_mask, cotangent, depth_kernel, norm_gain, up_weight, down_weight, layer_scale
):
    rows, cols, channels = fields.shape
    count = lax.axis_size("lon")
    cells = rows * cols
    hidden_width = up_weight.shape[1]
    factor = 1.0 / math.sqrt(cells * count)
    wide = jnp.float32
    in_vmem = pl.BlockSpec(memory_space=pltpu.VMEM)
    params = pltpu.CompilerParams(vmem_limit_bytes=VMEM_LIMIT)
    shape = functools.partial(jax.ShapeDtypeStruct, dtype=wide)
    shifted = pltpu.VMEM((7, rows + 6, cols, channels), wide)
    conv_cost = pl.CostEstimate(
        flops=100 * cells * channels, bytes_accessed=12 * cells * channels, transcendentals=0
    )

    masked = fields * sea_mask.astype(jnp.bfloat16)[:, :, None]
    mask = sea_mask.astype(wide)[:, :, None]
    ext = framed(masked, *halo(masked, count))
    taps = jnp.broadcast_to(depth_kernel.reshape(49, 1, channels), (49, 8, channels))

    nhat, istd = pl.pallas_call(
        forward_kernel,
        out_shape=(shape((rows, cols, channels)), shape((rows, cols, 1))),
        in_specs=[in_vmem] * 2,
        out_specs=(in_vmem, in_vmem),
        scratch_shapes=[shifted],
        compiler_params=params,
        cost_estimate=conv_cost,
        name="forward_conv",
    )(ext, taps)

    tile = 256
    by_cell = pl.BlockSpec((tile, channels), lambda i: (i, 0))
    one = pl.BlockSpec((tile, 1), lambda i: (i, 0))
    whole = lambda *dims: pl.BlockSpec(dims, lambda i: (0, 0))
    grad, terms = pl.pallas_call(
        functools.partial(mlp_kernel, factor),
        grid=(cells // tile,),
        out_shape=(
            shape((cells, channels)),
            jax.ShapeDtypeStruct((channels, 2 * hidden_width), jnp.bfloat16),
        ),
        in_specs=[
            by_cell,
            one,
            one,
            by_cell,
            whole(1, channels),
            whole(1, channels),
            whole(channels, hidden_width),
            whole(channels, hidden_width),
        ],
        out_specs=(by_cell, whole(channels, 2 * hidden_width)),
        scratch_shapes=[pltpu.VMEM((channels, hidden_width), wide)] * 2,
        compiler_params=params,
        cost_estimate=pl.CostEstimate(
            flops=10 * cells * channels * hidden_width,
            bytes_accessed=12 * cells * channels,
            transcendentals=cells * hidden_width,
        ),
        name="mlp",
    )(
        nhat.reshape(cells, channels),
        istd.reshape(cells, 1),
        mask.reshape(cells, 1),
        cotangent.reshape(cells, channels),
        norm_gain.reshape(1, channels),
        layer_scale.reshape(1, channels),
        up_weight,
        down_weight,
    )
    grad = grad.reshape(rows, cols, channels)
    around = halo(grad.astype(jnp.bfloat16), count)

    local_kernel = pl.pallas_call(
        functools.partial(taps_kernel, factor),
        out_shape=shape((7, 7, channels)),
        in_specs=[in_vmem] * 2,
        out_specs=in_vmem,
        scratch_shapes=[shifted],
        compiler_params=params,
        cost_estimate=conv_cost,
        name="kernel_grad",
    )(ext, grad)

    grad_fields = pl.pallas_call(
        back_kernel,
        out_shape=jax.ShapeDtypeStruct((rows, cols, channels), jnp.bfloat16),
        in_specs=[in_vmem] * 4,
        out_specs=in_vmem,
        scratch_shapes=[shifted, pltpu.VMEM((rows, cols, channels), wide)],
        compiler_params=params,
        cost_estimate=conv_cost,
        name="back_conv",
    )(framed(grad, *around), taps, mask, cotangent)

    local_kernel, grad_fields = lax.optimization_barrier((local_kernel, grad_fields))
    gathered = lax.all_gather(local_kernel, "lon")
    grad_kernel = jnp.sum(gathered, axis=0)
    arrived = lax.all_to_all(
        terms.reshape(count, channels // count, 2 * hidden_width), "lon", 0, 0
    )
    owned = jnp.sum(arrived.astype(wide), axis=0)
    return (grad_fields, grad_kernel, owned[:, :hidden_width], owned[:, hidden_width:])


def solution(mesh):
    return jax.shard_map(
        local,
        mesh=mesh,
        in_specs=(
            P("groups", "lon", None),
            P("groups", "lon"),
            P("groups", "lon", None),
            P(),
            P(),
            P(),
            P(),
            P(),
        ),
        out_specs=(
            P("groups", "lon", None),
            P("groups", None, None),
            P("lon", "groups"),
            P("lon", "groups"),
        ),
        check_vma=False,
    )
```
